32 devices in a mesh: dom: 2 (over x), ty: 4 (over y, core), tx: 4 (over z).
Axes of the slice: x: 2, y: 2, z: 4, core: 2. Of those that a mesh axis runs over, the one named last changes fastest.
Arguments:
- state: float32 [5, 4, 256, 512], P(None, None, ('dom', 'ty'), 'tx')
- vert_mix: float32 [256, 512], P(('dom', 'ty'), 'tx'), may hold values from 0.1 to 2
- fb_mask: int32 [256, 512], P(('dom', 'ty'), 'tx'), may hold values 0 or 1
- nu_coef: float32 [4, 5, 4], replicated, may hold values from 0.04 to 0.18
- adv_coef: float32 [4, 5, 4], replicated, may hold values from 0.05 to 0.2
- anchors: int32 [3, 2], replicated, may hold values from 0 to 256, as said below
Outputs:
- new_state: float32 [5, 4, 256, 512], P(None, None, ('dom', 'ty'), 'tx')
The draws below stay inside these ranges and needn't reach their ends.
Inputs may be any that keep to these rules, and one draw needn't show every extreme that they name: anchors[k] is the parent cell (row, column) where nest k+1's footprint of 32 x 512/2 parent cells begins; rows are multiples of 32, columns multiples of 128 up to 256; nest 1's row lies from 32 to 32, nests 2 and 3 take rows 0 and 32 in some order; column 0 and column 256 each occur in every draw; footprints may intersect.
All inputs are finite; a program needn't handle non-finite values. No bound on the sum of `fb_mask` on one device may be relied on, other than what follows from the above.
Results may differ from the reference program's by a relative error of at most 0.0003.
Values sent between devices are 32-bit elements; how exact they have to be, the bound alone decides.
A program may use at most 128 MiB of HBM per device.

```python
import math
import jax
import jax.numpy as jnp
from jax import lax

FIELDS = 5
LEVELS = 4
SUBSTEPS = 3
CY = 32
CX = 128
DY = 64
DX = 512
ROWS = 256


def draw_state(key, part):
    subkeys = jax.random.split(key, 1)
    full_shape = (FIELDS, LEVELS, ROWS, DX)
    return jax.random.normal(subkeys[0], full_shape, jnp.float32)


def draw_anchors(key, part):
    subkeys = jax.random.split(key, 4)
    row_top = DY // (2 * CY)
    col_top = DX // (2 * CX)
    first_row = jax.random.randint(subkeys[0], (1,), 1, row_top + 1).astype(jnp.int32)
    row_pair = jnp.stack([jnp.zeros((), jnp.int32), jnp.full((), row_top, jnp.int32)])
    pair_order = jax.random.permutation(subkeys[2], 2)
    row_steps = jnp.concatenate([first_row, row_pair[pair_order]])
    col_steps = jnp.stack([jnp.zeros((), jnp.int32), jnp.full((), col_top, jnp.int32), jax.random.randint(subkeys[1], (), 0, col_top + 1).astype(jnp.int32)])
    col_order = jax.random.permutation(subkeys[3], 3)
    return jnp.stack([row_steps * CY, col_steps[col_order] * CX], axis=1).astype(jnp.int32)


def set_ends(result, rng, low, largest):
    longest = result.shape.index(max(result.shape))
    spots = []
    for shift in (0, 1):
        where = [jax.random.randint(jax.random.fold_in(rng, axis), (), 0, length) for axis, length in enumerate(result.shape)]
        where[longest] = (where[longest] + shift) % result.shape[longest]
        spots.append(tuple(where))
    return result.at[spots[0]].set(low).at[spots[1]].set(largest)


def level_of(rng, extent, shards, smallest, high):
    gain = 1.0
    for position, blocks in shards:
        draws = jax.random.uniform(jax.random.fold_in(jax.random.fold_in(rng, 6), position), (blocks,), jnp.float32, smallest / len(shards), high / len(shards))
        gain = gain * jnp.repeat(jnp.exp(draws), extent[position] // blocks).reshape((-1,) + (1,) * (len(extent) - 1 - position))
    return gain


def setup_inputs(seed: int = 0) -> dict:
    splits = jax.random.split(jax.random.key(seed), 7)
    state = draw_state(jax.random.fold_in(splits[6], 71), 0)
    vert_mix = jnp.clip(jnp.exp(math.log(2.0) - 2.9957323 * jax.random.uniform(splits[1], (ROWS, DX), jnp.float32) ** level_of(splits[1], (ROWS, DX), ((0, 8), (1, 4)), -0.2, 0.2)), 0.1, 2.0)
    fb_mask = set_ends((jax.random.randint(splits[2], (ROWS, DX), 0, 4) < 3).astype(jnp.int32), jax.random.fold_in(splits[2], 1), 0, 1)
    nu_coef = jnp.clip(jax.random.uniform(splits[3], (4, FIELDS, LEVELS), jnp.float32, 0.04, 0.18), 0.04, 0.18)
    adv_coef = jnp.clip(jax.random.uniform(splits[4], (4, FIELDS, LEVELS), jnp.float32, 0.05, 0.2), 0.05, 0.2)
    anchors = draw_anchors(jax.random.fold_in(splits[6], 71), 0)
    return dict(state=state, vert_mix=vert_mix, fb_mask=fb_mask, nu_coef=nu_coef, adv_coef=adv_coef, anchors=anchors)


def spread_pairs(values):
    doubled = jnp.broadcast_to(values[..., None], values.shape + (2,))
    return doubled.reshape(values.shape[:-1] + (2 * values.shape[-1],))


def to_domains(values):
    leading = values.shape[:-2]
    count = len(leading)
    tiles = DY // CY
    shaped = values.reshape(leading + (2, tiles, 2, CY, DX))
    moved = jnp.moveaxis(shaped, (count, count + 2), (0, 1))
    return moved.reshape((4,) + leading + (DY, DX))


def from_domains(values):
    leading = values.shape[1:-2]
    count = len(leading)
    tiles = DY // CY
    shaped = values.reshape((2, 2) + leading + (tiles, CY, DX))
    moved = jnp.moveaxis(shaped, (0, 1), (count, count + 2))
    return moved.reshape(leading + (ROWS, DX))


def tridiagonal(explicit, mixing):
    nlevel = explicit.shape[1]
    cprime = []
    dprime = []
    for level_index in range(nlevel):
        ends = (1.0 if level_index == 0 else 0.0) + (1.0 if level_index == nlevel - 1 else 0.0)
        diagonal = 1.0 + mixing * (2.0 - ends)
        if level_index == 0:
            denom = diagonal
            dvalue = explicit[:, 0] / denom
        else:
            denom = diagonal + mixing * cprime[-1]
            dvalue = (explicit[:, level_index] + mixing * dprime[-1]) / denom
        cprime.append(-mixing / denom)
        dprime.append(dvalue)
    solved = [None] * nlevel
    solved[-1] = dprime[-1]
    for level_index in range(nlevel - 2, -1, -1):
        solved[level_index] = dprime[level_index] - cprime[level_index] * solved[level_index + 1]
    return jnp.stack(solved, axis=1)


def stencil_step(padded, mixing, diffusion, advection):
    center = padded[:, :, 1:-1, 1:-1]
    upper_cells = padded[:, :, :-2, 1:-1]
    lower_cells = padded[:, :, 2:, 1:-1]
    west_cells = padded[:, :, 1:-1, :-2]
    east_cells = padded[:, :, 1:-1, 2:]
    explicit = center + diffusion[:, :, None, None] * (upper_cells + lower_cells + west_cells + east_cells - 4.0 * center) + advection[:, :, None, None] * (west_cells - center)
    return tridiagonal(explicit, mixing)


def advance(fields, mixing, diffusion, advection, ghosts):
    padded = jnp.pad(fields, ((0, 0), (0, 0), (1, 1), (1, 1)))
    if ghosts is not None:
        padded = padded.at[:, :, 0, 1:-1].set(spread_pairs(ghosts[0]))
        padded = padded.at[:, :, -1, 1:-1].set(spread_pairs(ghosts[1]))
        padded = padded.at[:, :, 1:-1, 0].set(spread_pairs(ghosts[2]))
        padded = padded.at[:, :, 1:-1, -1].set(spread_pairs(ghosts[3]))
    return stencil_step(padded, mixing, diffusion, advection)


def footprint_edges(parent, anchor_row, anchor_col):
    zero_index = jnp.zeros((), jnp.int32)
    upper_row = lax.dynamic_slice(parent, (zero_index, zero_index, anchor_row, anchor_col), (FIELDS, LEVELS, 1, DX // 2))[:, :, 0]
    lower_row = lax.dynamic_slice(parent, (zero_index, zero_index, anchor_row + DY // 2 - 1, anchor_col), (FIELDS, LEVELS, 1, DX // 2))[:, :, 0]
    west_col = lax.dynamic_slice(parent, (zero_index, zero_index, anchor_row, anchor_col), (FIELDS, LEVELS, DY // 2, 1))[:, :, :, 0]
    east_col = lax.dynamic_slice(parent, (zero_index, zero_index, anchor_row, anchor_col + DX // 2 - 1), (FIELDS, LEVELS, DY // 2, 1))[:, :, :, 0]
    return (upper_row, lower_row, west_col, east_col)


def reference(state, vert_mix, fb_mask, nu_coef, adv_coef, anchors):
    parts = to_domains(state)
    mixes = to_domains(vert_mix)
    masks = to_domains(fb_mask).astype(jnp.float32)
    parent_old = parts[0]
    parent_new = advance(parent_old, mixes[0], nu_coef[0], adv_coef[0], None)
    finals = []
    for nest_number in range(3):
        domain = nest_number + 1
        anchor_row = anchors[nest_number, 0].astype(jnp.int32)
        anchor_col = anchors[nest_number, 1].astype(jnp.int32)
        old_edges = footprint_edges(parent_old, anchor_row, anchor_col)
        new_edges = footprint_edges(parent_new, anchor_row, anchor_col)
        fields = parts[domain]
        for substep in range(1, SUBSTEPS + 1):
            blend = (substep - 1) / SUBSTEPS
            if substep == 1:
                ghosts = old_edges
            else:
                ghosts = tuple(older + blend * (newer - older) for older, newer in zip(old_edges, new_edges))
            fields = advance(fields, mixes[domain], nu_coef[domain], adv_coef[domain], ghosts)
        finals.append(fields)
    sums = jnp.zeros((FIELDS, LEVELS, DY, DX), jnp.float32)
    counts = jnp.zeros((DY, DX), jnp.float32)
    zero_index = jnp.zeros((), jnp.int32)
    for nest_number in range(3):
        weights = masks[nest_number + 1]
        anchor_row = anchors[nest_number, 0].astype(jnp.int32)
        anchor_col = anchors[nest_number, 1].astype(jnp.int32)
        coarse_sums = (weights * finals[nest_number]).reshape(FIELDS, LEVELS, DY // 2, 2, DX // 2, 2).sum(axis=(3, 5))
        coarse_count = weights.reshape(DY // 2, 2, DX // 2, 2).sum(axis=(1, 3))
        start_four = (zero_index, zero_index, anchor_row, anchor_col)
        sums = lax.dynamic_update_slice(sums, lax.dynamic_slice(sums, start_four, (FIELDS, LEVELS, DY // 2, DX // 2)) + coarse_sums, start_four)
        counts = lax.dynamic_update_slice(counts, lax.dynamic_slice(counts, (anchor_row, anchor_col), (DY // 2, DX // 2)) + coarse_count, (anchor_row, anchor_col))
    accept = (masks[0] == 1.0) & (counts > 0.0)
    parent_out = jnp.where(accept, sums / jnp.maximum(counts, 1.0), parent_new)
    return from_domains(jnp.stack([parent_out] + finals))
```

```python
import functools

import jax
import jax.numpy as jnp
from jax import lax
from jax.experimental import pallas as pl
from jax.experimental.pallas import tpu as pltpu
from jax.sharding import PartitionSpec as P

SUBSTEPS = 3
VMEM_LIMIT = 32 << 20
MESH = pl.DeviceIdType.MESH


def repeat(count, body):
    if count <= 4:
        for index in range(count):
            body(index)
    else:

        def step(index, carry):
            body(index)
            return carry

        lax.fori_loop(0, count, step, 0)


def kernel(
    row_tiles,
    col_tiles,
    whole,
    mix,
    mask,
    nu,
    adv,
    anchors,
    out,
    state,
    current,
    packs,
    held,
    halo_rows,
    halo_cols,
    old_rows,
    new_rows,
    old_cols,
    new_cols,
    spread_rows,
    spread_cols,
    ghost_rows,
    ghost_cols,
    coef,
    piece,
    swapped,
    chosen,
    one_sums,
    slot_sums,
    load_sem,
    halo_send,
    halo_recv,
    tell_send,
    held_recv,
    edge_send,
    edge_recv,
    swap_sem,
    feed_send,
    one_recv,
    slot_recv,
):
    nfield, nlevel, nrow, ncol = state.shape
    count = nfield * nlevel
    padded = packs.shape[1] - nrow
    padded = padded // 2
    half = count // 2
    edge_rows, edge_cols = (old_rows, new_rows), (old_cols, new_cols)
    hrow, hcol = nrow // 2, ncol // 2
    half_rows = row_tiles // 2
    foot = half_rows // 2
    span = col_tiles // 2
    places = span + 1

    dom = lax.axis_index("dom")
    ty = lax.axis_index("ty")
    j = lax.axis_index("tx")
    parity = ty % 2
    i = ty // 2
    domain = 2 * dom + parity
    is_parent = domain == 0
    is_nest = domain > 0
    row_id = lax.broadcasted_iota(jnp.int32, (nrow, ncol), 0)
    lane = lax.broadcasted_iota(jnp.int32, (nrow, ncol), 1)

    def device(number, row, col):
        return (number // 2, 2 * row + number % 2, col)

    def copy(src, dst, send, recv, target):
        return pltpu.make_async_remote_copy(
            src_ref=src,
            dst_ref=dst,
            send_sem=send,
            recv_sem=recv,
            device_id=target,
            device_id_type=MESH,
        )

    fetch = pltpu.make_async_copy(whole, state, load_sem)
    fetch.start()
    barrier = pltpu.get_barrier_semaphore()

    def greet(target):
        pl.semaphore_signal(barrier, inc=1, device_id=target, device_id_type=MESH)

    greeted = jnp.int32(0)
    for there, row, col in (
        (i > 0, i - 1, j),
        (i < half_rows - 1, i + 1, j),
        (j > 0, i, j - 1),
        (j < col_tiles - 1, i, j + 1),
    ):
        greeted = greeted + there.astype(jnp.int32)

        @pl.when(there)
        def _():
            greet(device(domain, row, col))

    inside = half_rows > 2 and col_tiles > 2

    def greet_sources(row):
        def one(place):
            col = place + j // 2

            @pl.when((row != i) | (col != j))
            def _():
                greet(device(domain, row, col))

        repeat(places, one)

    @pl.when(is_parent)
    def _():
        for number in (1, 2, 3):
            greet(device(number, i, j))

        def nests(number, row_start, back):
            row_gap = i - row_start
            place = j - back

            @pl.when((row_gap >= 0) & (row_gap < foot) & (place >= 0) & (place < places))
            def _():
                for p in range(2):
                    for q in range(2):
                        row, col = 2 * row_gap + p, 2 * back + q

                        @pl.when(
                            (row > 0) & (row < half_rows - 1) & (col > 0) & (col < col_tiles - 1)
                        )
                        def _():
                            greet(device(number, row, col))

        if inside:
            for number in (2, 3):
                repeat(span, lambda back, number=number: nests(number, (i // foot) * foot, back))
            repeat(foot * span, lambda flat: nests(1, 1 + flat // span, flat % span))

    @pl.when(domain == 1)
    def _():
        greet(device(0, i, j))
        repeat(foot, lambda option: greet_sources(1 + option + i // 2))

    @pl.when(domain > 1)
    def _():
        greet(device(0, i, j))
        greet((dom, 2 * i + 1 - parity, j))
        repeat(2, lambda option: greet_sources(option * foot + i // 2))

    def pack(load, phase):
        packed = jnp.zeros((nrow, ncol), jnp.float32)
        for k in range(count):
            cells = load(k // nlevel, k % nlevel)
            packs[phase, k : k + 1, :] = cells[0:1, :]
            packs[phase, padded + k : padded + k + 1, :] = cells[nrow - 1 : nrow, :]
            rolled = pltpu.roll(cells, 2 * k + 1, 1)
            packed = jnp.where((lane == 2 * k) | (lane == 2 * k + 1), rolled, packed)
        if padded > count:
            rest = jnp.zeros((padded - count, ncol), jnp.float32)
            packs[phase, count:padded, :] = rest
            packs[phase, padded + count : 2 * padded, :] = rest
        packs[phase, 2 * padded :, :] = packed

    first_row = pl.ds(0, padded)
    last_row = pl.ds(padded, padded)
    side_cols = pl.ds(2 * padded, nrow)

    def halo(phase, act):
        moves = (
            (0, i < half_rows - 1, last_row, halo_rows, 0, i + 1, j, i > 0, i - 1, j),
            (1, i > 0, first_row, halo_rows, 1, i - 1, j, i < half_rows - 1, i + 1, j),
            (2, j < col_tiles - 1, side_cols, halo_cols, 0, i, j + 1, j > 0, i, j - 1),
            (3, j > 0, side_cols, halo_cols, 1, i, j - 1, j < col_tiles - 1, i, j + 1),
        )
        for way, sends, rows, buffer, side, row, col, takes, from_row, from_col in moves:

            def transfer(target, rows=rows, buffer=buffer, side=side, way=way):
                return copy(
                    packs.at[phase, rows],
                    buffer.at[phase, side],
                    halo_send.at[phase, way],
                    halo_recv.at[phase, way],
                    target,
                )

            if act == "start":

                @pl.when(sends)
                def _():
                    transfer(device(domain, row, col)).start()

            elif act == "recv":

                @pl.when(takes)
                def _():
                    transfer(device(domain, from_row, from_col)).wait_recv()

            else:

                @pl.when(sends)
                def _():
                    transfer(device(domain, row, col)).wait_send()

    def tell(phase, number):
        return copy(
            packs.at[phase],
            held.at[phase],
            tell_send.at[phase, number - 1],
            held_recv.at[phase],
            device(number, i, j),
        )

    def edges_out(phase, act):
        def one(option, row_start, back, index):
            row_gap = i - row_start
            place = j - back
            fits = (row_gap >= 0) & (row_gap < foot) & (place >= 0) & (place < places)
            slot = option * places + place
            for p in range(2):
                for q in range(2):
                    row = 2 * row_gap + p
                    col = 2 * back + q
                    here = (row == i) & (col == j)
                    spot = 4 * index + 2 * p + q

                    def go(rows, kind, buffer):
                        away = copy(
                            held.at[phase, rows],
                            buffer[phase].at[slot],
                            edge_send.at[phase, kind, spot],
                            edge_recv.at[phase, kind, slot],
                            device(domain, row, col),
                        )

                        @pl.when(jnp.logical_not(here))
                        def _():
                            if act == "start":
                                away.start()
                            else:
                                away.wait_send()

                        if act == "start":

                            @pl.when(here)
                            def _():
                                pltpu.make_async_copy(
                                    held.at[phase, rows],
                                    buffer[phase].at[slot],
                                    edge_recv.at[phase, kind, slot],
                                ).start()

                    @pl.when(fits & ((col == 0) | (col == col_tiles - 1)))
                    def _():
                        go(pl.ds(2 * padded + p * hrow, hrow), 1, edge_cols)

                    @pl.when(fits & (row == 0))
                    def _():
                        go(first_row, 0, edge_rows)

                    @pl.when(fits & (row == half_rows - 1))
                    def _():
                        go(last_row, 0, edge_rows)

        @pl.when(domain > 1)
        def _():
            option = i // foot
            repeat(span, lambda back: one(option, option * foot, back, back))

        @pl.when(domain == 1)
        def _():
            repeat(
                foot * span,
                lambda flat: one(flat // span, 1 + flat // span, flat % span, flat),
            )

    at_row_end = (i == 0) | (i == half_rows - 1)
    at_col_end = (j == 0) | (j == col_tiles - 1)
    number_here = jnp.maximum(domain - 1, 0)
    row_here = anchors[0, number_here] // nrow
    col_here = anchors[1, number_here] // ncol
    option_here = jnp.where(domain == 1, row_here - 1, row_here // foot)
    slot_here = jnp.clip(option_here * places + col_here, 0, old_rows.shape[0] - 1)

    def edges_in(phase):
        def wait(slot):
            away = device(0, i // 2, j // 2)

            @pl.when(at_row_end)
            def _():
                copy(
                    packs.at[phase, first_row],
                    edge_rows[phase].at[slot],
                    edge_send.at[phase, 0, 0],
                    edge_recv.at[phase, 0, slot],
                    away,
                ).wait_recv()

            @pl.when(at_col_end)
            def _():
                copy(
                    packs.at[phase, pl.ds(2 * padded, hrow)],
                    edge_cols[phase].at[slot],
                    edge_send.at[phase, 1, 0],
                    edge_recv.at[phase, 1, slot],
                    away,
                ).wait_recv()

        @pl.when(domain == 1)
        def _():
            repeat(foot * places, wait)

        @pl.when(domain > 1)
        def _():
            repeat(2 * places, wait)

        @pl.when(at_row_end)
        def _():
            source = lax.broadcasted_iota(jnp.int32, (ncol, ncol), 0)
            target = lax.broadcasted_iota(jnp.int32, (ncol, ncol), 1)
            spread = (source == (j % 2) * hcol + target // 2).astype(jnp.float32)
            spread_rows[phase] = jnp.dot(
                edge_rows[phase][slot_here],
                spread,
                precision=lax.Precision.HIGHEST,
                preferred_element_type=jnp.float32,
            )

        @pl.when(at_col_end)
        def _():
            values = edge_cols[phase][slot_here]
            spread_cols[phase, pl.ds(0, hrow, stride=2), :] = values
            spread_cols[phase, pl.ds(1, hrow, stride=2), :] = values

    def ghosts(phase):
        def blended(values):
            if phase == 0:
                return values[0]
            return values[0] + (phase / SUBSTEPS) * (values[1] - values[0])

        for side, inner in ((0, i > 0), (1, i < half_rows - 1)):

            @pl.when(inner)
            def _():
                ghost_rows[side] = halo_rows[phase, side]

            @pl.when(jnp.logical_not(inner) & is_nest)
            def _():
                ghost_rows[side] = blended(spread_rows)

            @pl.when(jnp.logical_not(inner) & is_parent)
            def _():
                ghost_rows[side] = jnp.zeros((padded, ncol), jnp.float32)

        for side, inner in ((0, j > 0), (1, j < col_tiles - 1)):

            @pl.when(inner)
            def _():
                ghost_cols[side] = halo_cols[phase, side]

            @pl.when(jnp.logical_not(inner) & is_nest)
            def _():
                shift = ncol - 1 if side == 0 else 1
                ghost_cols[side] = pltpu.roll(blended(spread_cols), shift, 1)

            @pl.when(jnp.logical_not(inner) & is_parent)
            def _():
                ghost_cols[side] = jnp.zeros((nrow, ncol), jnp.float32)

    def advance(load, store):
        sides = jnp.where(lane % 2 == 0, ghost_cols[0], ghost_cols[1])
        mixing = mix[...]
        for f in range(nfield):
            forward = []
            for level in range(nlevel):
                k = f * nlevel + level
                cells = load(f, level)
                diffusion = nu[domain, level, f]
                advection = adv[domain, level, f]
                above = jnp.where(
                    row_id == 0, ghost_rows[0, k : k + 1, :], pltpu.roll(cells, 1, 0)
                )
                below = jnp.where(
                    row_id == nrow - 1,
                    ghost_rows[1, k : k + 1, :],
                    pltpu.roll(cells, nrow - 1, 0),
                )
                beside = pltpu.roll(sides, (ncol - 2 * k - 1) % ncol, 1)
                west = pltpu.roll(jnp.where(lane == ncol - 1, beside, cells), 1, 1)
                east = pltpu.roll(jnp.where(lane == 0, beside, cells), ncol - 1, 1)
                explicit = (
                    cells
                    + diffusion * (above + below + west + east - 4.0 * cells)
                    + advection * (west - cells)
                )
                if level == 0:
                    forward.append(explicit * coef[level])
                else:
                    forward.append((explicit + mixing * forward[-1]) * coef[level])
            solved = forward[-1]
            store(f, nlevel - 1, solved)
            for level in range(nlevel - 2, -1, -1):
                solved = forward[level] + coef[nlevel + level] * solved
                store(f, level, solved)

    def put(buffer, *prefix):
        def store(f, level, values):
            buffer[(*prefix, f, level)] = values

        return store

    def get(buffer, *prefix):
        return lambda f, level: buffer[(*prefix, f, level)]

    mixing = mix[...]
    ratio = None
    for level in range(nlevel):
        ends = (1.0 if level == 0 else 0.0) + (1.0 if level == nlevel - 1 else 0.0)
        pivot = 1.0 + mixing * (2.0 - ends)
        if level > 0:
            pivot = pivot - mixing * ratio
        inverse = 1.0 / pivot
        ratio = mixing * inverse
        coef[level] = inverse
        coef[nlevel + level] = ratio

    fetch.wait()
    pack(get(state), 0)
    backs = jnp.minimum(span - 1, j) - jnp.maximum(0, j - span) + 1
    gaps = jnp.minimum(foot - 1, i - 1) - jnp.maximum(0, i - foot) + 1
    option_start = (i // foot) * foot
    lone = jnp.where(domain == 1, i >= 1, option_start == i - i // 2).astype(jnp.int32)
    targets = 4 * backs * jnp.where(domain == 1, gaps, 1) - lone
    if inside:
        deep = jnp.logical_not(at_row_end | at_col_end).astype(jnp.int32)
        targets = targets + deep * places * jnp.where(domain == 1, foot, 2)
    partners = jnp.where(is_parent, 3, 1 + targets + jnp.where(domain == 1, 0, 1))
    pl.semaphore_wait(barrier, greeted + partners)

    def relay(phase):
        tell(phase, 1).wait_recv()
        edges_out(phase, "start")

    @pl.when(is_parent)
    def _():
        for number in (1, 2, 3):
            tell(0, number).start()

    halo(0, "start")

    @pl.when(is_nest)
    def _():
        relay(0)

    halo(0, "recv")

    @pl.when(is_nest)
    def _():
        relay(1)
        edges_in(0)

    ghosts(0)
    advance(get(state), put(current, 0))
    pack(get(current, 0), 1)

    @pl.when(is_parent)
    def _():
        for number in (1, 2, 3):
            tell(1, number).start()

    feeds = foot * places

    def feed_one(flat):
        option = flat // places
        place = flat % places
        where_to = device(0, 1 + option + i // 2, place + j // 2)
        part = 2 * (i % 2) + j % 2
        return copy(
            chosen,
            one_sums.at[flat, part],
            feed_send.at[flat],
            one_recv.at[flat, part],
            where_to,
        )

    def feed_slot(place):
        where_to = device(0, parity * foot + i // 2, place + j // 2)
        part = 2 * (i % 2) + j % 2
        return copy(
            chosen,
            slot_sums.at[place, part],
            feed_send.at[place],
            slot_recv.at[place, part],
            where_to,
        )

    def swap():
        return copy(
            piece, swapped, swap_sem.at[0], swap_sem.at[1], (dom, 2 * i + 1 - parity, j)
        )

    @pl.when(is_nest)
    def _():
        halo(1, "start")
        halo(1, "recv")
        edges_in(1)
        ghosts(1)
        advance(get(current, 0), put(current, 1))
        pack(get(current, 1), 2)
        halo(2, "start")
        halo(2, "recv")
        ghosts(2)
        advance(get(current, 1), put(out))
        source = lax.broadcasted_iota(jnp.int32, (2 * ncol, ncol), 0)
        target = lax.broadcasted_iota(jnp.int32, (2 * ncol, ncol), 1)
        gather = (target == source // 2).astype(jnp.float32)
        even = mask[pl.ds(0, hrow, stride=2), :].astype(jnp.float32)
        odd = mask[pl.ds(1, hrow, stride=2), :].astype(jnp.float32)

        def pairs(k):
            f, level = k // nlevel, k % nlevel
            return (
                even * out[f, level, pl.ds(0, hrow, stride=2), :]
                + odd * out[f, level, pl.ds(1, hrow, stride=2), :]
            )

        tall = []
        for k in range(half):
            tall.append(jnp.concatenate([pairs(k), pairs(k + half)], axis=1))
        tall.append(jnp.concatenate([even + odd, jnp.zeros_like(even)], axis=1))
        piece[...] = jnp.dot(
            jnp.concatenate(tall, axis=0),
            gather,
            precision=lax.Precision.HIGHEST,
            preferred_element_type=jnp.float32,
        )

        @pl.when(domain == 1)
        def _():
            chosen[...] = piece[...]
            repeat(feeds, lambda flat: feed_one(flat).start())

        @pl.when(domain > 1)
        def _():
            swap().start()
            swap().wait_recv()
            mine = row_here == parity * foot
            chosen[...] = jnp.where(mine, piece[...], swapped[...])
            repeat(places, lambda place: feed_slot(place).start())

    @pl.when(is_parent)
    def _():
        away = device(1, i // 2, j // 2)

        def take_one(flat):
            option = flat // places
            place = flat % places
            row_gap = i - 1 - option
            back = j - place

            @pl.when((row_gap >= 0) & (row_gap < foot) & (back >= 0) & (back < span))
            def _():
                for part in range(4):
                    copy(
                        chosen,
                        one_sums.at[flat, part],
                        feed_send.at[0],
                        one_recv.at[flat, part],
                        away,
                    ).wait_recv()

        def take_slot(place):
            back = j - place

            @pl.when((back >= 0) & (back < span))
            def _():
                for part in range(4):
                    copy(
                        chosen,
                        slot_sums.at[place, part],
                        feed_send.at[0],
                        slot_recv.at[place, part],
                        away,
                    ).wait_recv()

        repeat(feeds, take_one)
        repeat(places, take_slot)
        one_row = anchors[0, 0] // nrow
        one_col = anchors[1, 0] // ncol
        slot = i // foot
        second = anchors[0, 1] // nrow == slot * foot
        slot_col = jnp.where(second, anchors[1, 1], anchors[1, 2]) // ncol
        slot_at = jnp.clip(slot_col, 0, places - 1)
        one_in = (i >= one_row) & (i < one_row + foot) & (j >= one_col) & (j < one_col + span)
        slot_in = (j >= slot_col) & (j < slot_col + span)
        one_at = jnp.clip((one_row - 1) * places + one_col, 0, feeds - 1)
        left = lax.broadcasted_iota(jnp.int32, (hrow, ncol), 1) < hcol

        def both(part, rows):
            one = one_sums[one_at, part, rows, :]
            other = slot_sums[slot_at, part, rows, :]
            return jnp.where(one_in, one, 0.0) + jnp.where(slot_in, other, 0.0)

        for p in range(2):
            here = slice(p * hrow, (p + 1) * hrow)
            rows = slice(half * hrow, (half + 1) * hrow)
            total = jnp.where(
                left, both(2 * p, rows), pltpu.roll(both(2 * p + 1, rows), hcol, 1)
            )
            accept = (mask[here, :] == 1) & (total > 0.0)
            scale = 1.0 / jnp.maximum(total, 1.0)
            for k in range(half):
                rows = slice(k * hrow, (k + 1) * hrow)
                near = both(2 * p, rows)
                far = both(2 * p + 1, rows)
                low = jnp.where(left, near, pltpu.roll(far, hcol, 1))
                high = jnp.where(left, pltpu.roll(near, hcol, 1), far)
                for field, sums in ((k, low), (k + half, high)):
                    f, level = field // nlevel, field % nlevel
                    out[f, level, here, :] = jnp.where(
                        accept, sums * scale, current[0, f, level, here, :]
                    )

    halo(0, "send")

    @pl.when(is_parent)
    def _():
        for phase in range(2):
            for number in (1, 2, 3):
                tell(phase, number).wait_send()

    @pl.when(is_nest)
    def _():
        halo(1, "send")
        halo(2, "send")
        edges_out(0, "send")
        edges_out(1, "send")

        @pl.when(domain == 1)
        def _():
            repeat(feeds, lambda flat: feed_one(flat).wait_send())

        @pl.when(domain > 1)
        def _():
            swap().wait_send()
            repeat(places, lambda place: feed_slot(place).wait_send())


def shards(row_tiles, col_tiles, state, vert_mix, fb_mask, nu_coef, adv_coef, anchors):
    nfield, nlevel, nrow, ncol = state.shape
    count = nfield * nlevel
    padded = -(-count // 8) * 8
    foot = row_tiles // 4
    span = col_tiles // 2
    places = span + 1
    options = max(foot, 2)
    tall = (count // 2 + 1) * (nrow // 2)
    sent = 4 * foot * span
    f32 = jnp.float32
    vmem = pl.BlockSpec(memory_space=pltpu.VMEM)
    smem = pl.BlockSpec(memory_space=pltpu.SMEM)
    dma = pltpu.SemaphoreType.DMA
    return pl.pallas_call(
        functools.partial(kernel, row_tiles, col_tiles),
        out_shape=jax.ShapeDtypeStruct(state.shape, f32),
        in_specs=[pl.BlockSpec(memory_space=pltpu.HBM), vmem, vmem, smem, smem, smem],
        out_specs=vmem,
        scratch_shapes=[
            pltpu.VMEM(state.shape, f32),
            pltpu.VMEM((2, nfield, nlevel, nrow, ncol), f32),
            pltpu.VMEM((3, 2 * padded + nrow, ncol), f32),
            pltpu.VMEM((2, 2 * padded + nrow, ncol), f32),
            pltpu.VMEM((3, 2, padded, ncol), f32),
            pltpu.VMEM((3, 2, nrow, ncol), f32),
            pltpu.VMEM((options * places, padded, ncol), f32),
            pltpu.VMEM((options * places, padded, ncol), f32),
            pltpu.VMEM((options * places, nrow // 2, ncol), f32),
            pltpu.VMEM((options * places, nrow // 2, ncol), f32),
            pltpu.VMEM((2, padded, ncol), f32),
            pltpu.VMEM((2, nrow, ncol), f32),
            pltpu.VMEM((2, padded, ncol), f32),
            pltpu.VMEM((2, nrow, ncol), f32),
            pltpu.VMEM((2 * nlevel, nrow, ncol), f32),
            pltpu.VMEM((tall, ncol), f32),
            pltpu.VMEM((tall, ncol), f32),
            pltpu.VMEM((tall, ncol), f32),
            pltpu.VMEM((foot * places, 4, tall, ncol), f32),
            pltpu.VMEM((places, 4, tall, ncol), f32),
            dma,
            dma((3, 4)),
            dma((3, 4)),
            dma((2, 3)),
            dma((2,)),
            dma((2, 2, sent)),
            dma((2, 2, options * places)),
            dma((2,)),
            dma((foot * places,)),
            dma((foot * places, 4)),
            dma((places, 4)),
        ],
        compiler_params=pltpu.CompilerParams(
            has_side_effects=True, collective_id=0, vmem_limit_bytes=VMEM_LIMIT
        ),
    )(
        state,
        vert_mix,
        fb_mask,
        jnp.swapaxes(nu_coef, 1, 2),
        jnp.swapaxes(adv_coef, 1, 2),
        jnp.swapaxes(anchors, 0, 1),
    )


def solution(mesh):
    in_specs = (
        P(None, None, ("dom", "ty"), "tx"),
        P(("dom", "ty"), "tx"),
        P(("dom", "ty"), "tx"),
        P(),
        P(),
        P(),
    )
    out_specs = P(None, None, ("dom", "ty"), "tx")
    body = functools.partial(shards, mesh.shape["ty"], mesh.shape["tx"])
    return jax.shard_map(body, mesh=mesh, in_specs=in_specs, out_specs=out_specs, check_vma=False)
```

```python
import functools

import jax
import jax.numpy as jnp
from jax import lax
from jax.experimental import pallas as pl
from jax.experimental.pallas import tpu as pltpu
from jax.sharding import PartitionSpec as P

SUBSTEPS = 3
VMEM_LIMIT = 32 << 20
MESH = pl.DeviceIdType.MESH


def repeat(count, body):
    if count <= 4:
        for index in range(count):
            body(index)
    else:

        def step(index, carry):
            body(index)
            return carry

        lax.fori_loop(0, count, step, 0)


def kernel(
    row_tiles,
    col_tiles,
    whole,
    mix_in,
    mask_in,
    nu_in,
    adv_in,
    anchors_in,
    out,
    state,
    mix,
    mask,
    nu,
    adv,
    anchors,
    current,
    packs,
    held,
    halo_rows,
    halo_cols,
    old_rows,
    new_rows,
    old_cols,
    new_cols,
    spread_rows,
    spread_cols,
    ghost_rows,
    ghost_cols,
    coef,
    piece,
    swapped,
    chosen,
    one_sums,
    slot_sums,
    load_sem,
    halo_send,
    halo_recv,
    tell_send,
    held_recv,
    edge_send,
    edge_recv,
    swap_sem,
    feed_send,
    one_recv,
    slot_recv,
):
    nfield, nlevel, nrow, ncol = state.shape
    count = nfield * nlevel
    padded = packs.shape[1] - nrow
    padded = padded // 2
    half = count // 2
    edge_rows, edge_cols = (old_rows, new_rows), (old_cols, new_cols)
    hrow, hcol = nrow // 2, ncol // 2
    half_rows = row_tiles // 2
    foot = half_rows // 2
    span = col_tiles // 2
    places = span + 1

    dom = lax.axis_index("dom")
    ty = lax.axis_index("ty")
    j = lax.axis_index("tx")
    parity = ty % 2
    i = ty // 2
    domain = 2 * dom + parity
    is_parent = domain == 0
    is_nest = domain > 0
    row_id = lax.broadcasted_iota(jnp.int32, (nrow, ncol), 0)
    lane = lax.broadcasted_iota(jnp.int32, (nrow, ncol), 1)

    def device(number, row, col):
        return (number // 2, 2 * row + number % 2, col)

    def copy(src, dst, send, recv, target):
        return pltpu.make_async_remote_copy(
            src_ref=src,
            dst_ref=dst,
            send_sem=send,
            recv_sem=recv,
            device_id=target,
            device_id_type=MESH,
        )

    loads = [
        pltpu.make_async_copy(source, target, load_sem.at[index])
        for index, (source, target) in enumerate(
            (
                (whole, state),
                (mix_in, mix),
                (mask_in, mask),
                (nu_in, nu),
                (adv_in, adv),
                (anchors_in, anchors),
            )
        )
    ]
    for load in loads:
        load.start()
    barrier = pltpu.get_barrier_semaphore()

    def greet(target):
        pl.semaphore_signal(barrier, inc=1, device_id=target, device_id_type=MESH)

    greeted = jnp.int32(0)
    for there, row, col in (
        (i > 0, i - 1, j),
        (i < half_rows - 1, i + 1, j),
        (j > 0, i, j - 1),
        (j < col_tiles - 1, i, j + 1),
    ):
        greeted = greeted + there.astype(jnp.int32)

        @pl.when(there)
        def _():
            greet(device(domain, row, col))

    inside = half_rows > 2 and col_tiles > 2

    def greet_sources(row):
        def one(place):
            col = place + j // 2

            @pl.when((row != i) | (col != j))
            def _():
                greet(device(domain, row, col))

        repeat(places, one)

    @pl.when(is_parent)
    def _():
        for number in (1, 2, 3):
            greet(device(number, i, j))

        def nests(number, row_start, back):
            row_gap = i - row_start
            place = j - back

            @pl.when((row_gap >= 0) & (row_gap < foot) & (place >= 0) & (place < places))
            def _():
                for p in range(2):
                    for q in range(2):
                        row, col = 2 * row_gap + p, 2 * back + q

                        @pl.when(
                            (row > 0) & (row < half_rows - 1) & (col > 0) & (col < col_tiles - 1)
                        )
                        def _():
                            greet(device(number, row, col))

        if inside:
            for number in (2, 3):
                repeat(span, lambda back, number=number: nests(number, (i // foot) * foot, back))
            repeat(foot * span, lambda flat: nests(1, 1 + flat // span, flat % span))

    @pl.when(domain == 1)
    def _():
        greet(device(0, i, j))
        repeat(foot, lambda option: greet_sources(1 + option + i // 2))

    @pl.when(domain > 1)
    def _():
        greet(device(0, i, j))
        greet((dom, 2 * i + 1 - parity, j))
        repeat(2, lambda option: greet_sources(option * foot + i // 2))

    def pack(load, phase):
        packed = jnp.zeros((nrow, ncol), jnp.float32)
        for k in range(count):
            cells = load(k // nlevel, k % nlevel)
            packs[phase, k : k + 1, :] = cells[0:1, :]
            packs[phase, padded + k : padded + k + 1, :] = cells[nrow - 1 : nrow, :]
            rolled = pltpu.roll(cells, 2 * k + 1, 1)
            packed = jnp.where((lane == 2 * k) | (lane == 2 * k + 1), rolled, packed)
        if padded > count:
            rest = jnp.zeros((padded - count, ncol), jnp.float32)
            packs[phase, count:padded, :] = rest
            packs[phase, padded + count : 2 * padded, :] = rest
        packs[phase, 2 * padded :, :] = packed

    first_row = pl.ds(0, padded)
    last_row = pl.ds(padded, padded)
    side_cols = pl.ds(2 * padded, nrow)

    def halo(phase, act):
        moves = (
            (0, i < half_rows - 1, last_row, halo_rows, 0, i + 1, j, i > 0, i - 1, j),
            (1, i > 0, first_row, halo_rows, 1, i - 1, j, i < half_rows - 1, i + 1, j),
            (2, j < col_tiles - 1, side_cols, halo_cols, 0, i, j + 1, j > 0, i, j - 1),
            (3, j > 0, side_cols, halo_cols, 1, i, j - 1, j < col_tiles - 1, i, j + 1),
        )
        for way, sends, rows, buffer, side, row, col, takes, from_row, from_col in moves:

            def transfer(target, rows=rows, buffer=buffer, side=side, way=way):
                return copy(
                    packs.at[phase, rows],
                    buffer.at[phase, side],
                    halo_send.at[phase, way],
                    halo_recv.at[phase, way],
                    target,
                )

            if act == "start":

                @pl.when(sends)
                def _():
                    transfer(device(domain, row, col)).start()

            elif act == "recv":

                @pl.when(takes)
                def _():
                    transfer(device(domain, from_row, from_col)).wait_recv()

            else:

                @pl.when(sends)
                def _():
                    transfer(device(domain, row, col)).wait_send()

    def tell(phase, number):
        return copy(
            packs.at[phase],
            held.at[phase],
            tell_send.at[phase, number - 1],
            held_recv.at[phase],
            device(number, i, j),
        )

    def edges_out(phase, act):
        def one(option, row_start, back, index):
            row_gap = i - row_start
            place = j - back
            fits = (row_gap >= 0) & (row_gap < foot) & (place >= 0) & (place < places)
            slot = option * places + place
            for p in range(2):
                for q in range(2):
                    row = 2 * row_gap + p
                    col = 2 * back + q
                    here = (row == i) & (col == j)
                    spot = 4 * index + 2 * p + q

                    def go(rows, kind, buffer):
                        away = copy(
                            held.at[phase, rows],
                            buffer[phase].at[slot],
                            edge_send.at[phase, kind, spot],
                            edge_recv.at[phase, kind, slot],
                            device(domain, row, col),
                        )

                        @pl.when(jnp.logical_not(here))
                        def _():
                            if act == "start":
                                away.start()
                            else:
                                away.wait_send()

                        if act == "start":

                            @pl.when(here)
                            def _():
                                pltpu.make_async_copy(
                                    held.at[phase, rows],
                                    buffer[phase].at[slot],
                                    edge_recv.at[phase, kind, slot],
                                ).start()

                    @pl.when(fits & ((col == 0) | (col == col_tiles - 1)))
                    def _():
                        go(pl.ds(2 * padded + p * hrow, hrow), 1, edge_cols)

                    @pl.when(fits & (row == 0))
                    def _():
                        go(first_row, 0, edge_rows)

                    @pl.when(fits & (row == half_rows - 1))
                    def _():
                        go(last_row, 0, edge_rows)

        @pl.when(domain > 1)
        def _():
            option = i // foot
            repeat(span, lambda back: one(option, option * foot, back, back))

        @pl.when(domain == 1)
        def _():
            repeat(
                foot * span,
                lambda flat: one(flat // span, 1 + flat // span, flat % span, flat),
            )

    at_row_end = (i == 0) | (i == half_rows - 1)
    at_col_end = (j == 0) | (j == col_tiles - 1)
    def find_slot():
        number_here = jnp.maximum(domain - 1, 0)
        row_here = anchors[0, number_here] // nrow
        col_here = anchors[1, number_here] // ncol
        option_here = jnp.where(domain == 1, row_here - 1, row_here // foot)
        slot = option_here * places + col_here
        return row_here, jnp.clip(slot, 0, old_rows.shape[0] - 1)

    def edges_in(phase):
        def wait(slot):
            away = device(0, i // 2, j // 2)

            @pl.when(at_row_end)
            def _():
                copy(
                    packs.at[phase, first_row],
                    edge_rows[phase].at[slot],
                    edge_send.at[phase, 0, 0],
                    edge_recv.at[phase, 0, slot],
                    away,
                ).wait_recv()

            @pl.when(at_col_end)
            def _():
                copy(
                    packs.at[phase, pl.ds(2 * padded, hrow)],
                    edge_cols[phase].at[slot],
                    edge_send.at[phase, 1, 0],
                    edge_recv.at[phase, 1, slot],
                    away,
                ).wait_recv()

        @pl.when(domain == 1)
        def _():
            repeat(foot * places, wait)

        @pl.when(domain > 1)
        def _():
            repeat(2 * places, wait)

        row_here, slot_here = find_slot()

        @pl.when(at_row_end)
        def _():
            source = lax.broadcasted_iota(jnp.int32, (ncol, ncol), 0)
            target = lax.broadcasted_iota(jnp.int32, (ncol, ncol), 1)
            spread = (source == (j % 2) * hcol + target // 2).astype(jnp.float32)
            spread_rows[phase] = jnp.dot(
                edge_rows[phase][slot_here],
                spread,
                precision=lax.Precision.HIGHEST,
                preferred_element_type=jnp.float32,
            )

        @pl.when(at_col_end)
        def _():
            values = edge_cols[phase][slot_here]
            spread_cols[phase, pl.ds(0, hrow, stride=2), :] = values
            spread_cols[phase, pl.ds(1, hrow, stride=2), :] = values

    def ghosts(phase):
        def blended(values):
            if phase == 0:
                return values[0]
            return values[0] + (phase / SUBSTEPS) * (values[1] - values[0])

        for side, inner in ((0, i > 0), (1, i < half_rows - 1)):

            @pl.when(inner)
            def _():
                ghost_rows[side] = halo_rows[phase, side]

            @pl.when(jnp.logical_not(inner) & is_nest)
            def _():
                ghost_rows[side] = blended(spread_rows)

            @pl.when(jnp.logical_not(inner) & is_parent)
            def _():
                ghost_rows[side] = jnp.zeros((padded, ncol), jnp.float32)

        for side, inner in ((0, j > 0), (1, j < col_tiles - 1)):

            @pl.when(inner)
            def _():
                ghost_cols[side] = halo_cols[phase, side]

            @pl.when(jnp.logical_not(inner) & is_nest)
            def _():
                shift = ncol - 1 if side == 0 else 1
                ghost_cols[side] = pltpu.roll(blended(spread_cols), shift, 1)

            @pl.when(jnp.logical_not(inner) & is_parent)
            def _():
                ghost_cols[side] = jnp.zeros((nrow, ncol), jnp.float32)

    def advance(load, store):
        sides = jnp.where(lane % 2 == 0, ghost_cols[0], ghost_cols[1])
        mixing = mix[...]
        for f in range(nfield):
            forward = []
            for level in range(nlevel):
                k = f * nlevel + level
                cells = load(f, level)
                diffusion = nu[domain, level, f]
                advection = adv[domain, level, f]
                above = jnp.where(
                    row_id == 0, ghost_rows[0, k : k + 1, :], pltpu.roll(cells, 1, 0)
                )
                below = jnp.where(
                    row_id == nrow - 1,
                    ghost_rows[1, k : k + 1, :],
                    pltpu.roll(cells, nrow - 1, 0),
                )
                beside = pltpu.roll(sides, (ncol - 2 * k - 1) % ncol, 1)
                west = pltpu.roll(jnp.where(lane == ncol - 1, beside, cells), 1, 1)
                east = pltpu.roll(jnp.where(lane == 0, beside, cells), ncol - 1, 1)
                explicit = (
                    cells
                    + diffusion * (above + below + west + east - 4.0 * cells)
                    + advection * (west - cells)
                )
                if level == 0:
                    forward.append(explicit * coef[level])
                else:
                    forward.append((explicit + mixing * forward[-1]) * coef[level])
            solved = forward[-1]
            store(f, nlevel - 1, solved)
            for level in range(nlevel - 2, -1, -1):
                solved = forward[level] + coef[nlevel + level] * solved
                store(f, level, solved)

    def put(buffer, *prefix):
        def store(f, level, values):
            buffer[(*prefix, f, level)] = values

        return store

    def get(buffer, *prefix):
        return lambda f, level: buffer[(*prefix, f, level)]

    for load in loads[1:]:
        load.wait()
    mixing = mix[...]
    ratio = None
    for level in range(nlevel):
        ends = (1.0 if level == 0 else 0.0) + (1.0 if level == nlevel - 1 else 0.0)
        pivot = 1.0 + mixing * (2.0 - ends)
        if level > 0:
            pivot = pivot - mixing * ratio
        inverse = 1.0 / pivot
        ratio = mixing * inverse
        coef[level] = inverse
        coef[nlevel + level] = ratio

    loads[0].wait()
    pack(get(state), 0)
    backs = jnp.minimum(span - 1, j) - jnp.maximum(0, j - span) + 1
    gaps = jnp.minimum(foot - 1, i - 1) - jnp.maximum(0, i - foot) + 1
    option_start = (i // foot) * foot
    lone = jnp.where(domain == 1, i >= 1, option_start == i - i // 2).astype(jnp.int32)
    targets = 4 * backs * jnp.where(domain == 1, gaps, 1) - lone
    if inside:
        deep = jnp.logical_not(at_row_end | at_col_end).astype(jnp.int32)
        targets = targets + deep * places * jnp.where(domain == 1, foot, 2)
    partners = jnp.where(is_parent, 3, 1 + targets + jnp.where(domain == 1, 0, 1))
    pl.semaphore_wait(barrier, greeted + partners)

    def relay(phase):
        tell(phase, 1).wait_recv()
        edges_out(phase, "start")

    @pl.when(is_parent)
    def _():
        for number in (1, 2, 3):
            tell(0, number).start()

    halo(0, "start")

    @pl.when(is_nest)
    def _():
        relay(0)

    halo(0, "recv")

    @pl.when(is_nest)
    def _():
        relay(1)
        edges_in(0)

    ghosts(0)
    advance(get(state), put(current, 0))
    pack(get(current, 0), 1)

    @pl.when(is_parent)
    def _():
        for number in (1, 2, 3):
            tell(1, number).start()

    feeds = foot * places

    def feed_one(flat):
        option = flat // places
        place = flat % places
        where_to = device(0, 1 + option + i // 2, place + j // 2)
        part = 2 * (i % 2) + j % 2
        return copy(
            chosen,
            one_sums.at[flat, part],
            feed_send.at[flat],
            one_recv.at[flat, part],
            where_to,
        )

    def feed_slot(place):
        where_to = device(0, parity * foot + i // 2, place + j // 2)
        part = 2 * (i % 2) + j % 2
        return copy(
            chosen,
            slot_sums.at[place, part],
            feed_send.at[place],
            slot_recv.at[place, part],
            where_to,
        )

    def swap():
        return copy(
            piece, swapped, swap_sem.at[0], swap_sem.at[1], (dom, 2 * i + 1 - parity, j)
        )

    @pl.when(is_nest)
    def _():
        halo(1, "start")
        halo(1, "recv")
        edges_in(1)
        ghosts(1)
        advance(get(current, 0), put(current, 1))
        pack(get(current, 1), 2)
        halo(2, "start")
        halo(2, "recv")
        ghosts(2)
        advance(get(current, 1), put(out))
        source = lax.broadcasted_iota(jnp.int32, (2 * ncol, ncol), 0)
        target = lax.broadcasted_iota(jnp.int32, (2 * ncol, ncol), 1)
        gather = (target == source // 2).astype(jnp.float32)
        even = mask[pl.ds(0, hrow, stride=2), :].astype(jnp.float32)
        odd = mask[pl.ds(1, hrow, stride=2), :].astype(jnp.float32)

        def pairs(k):
            f, level = k // nlevel, k % nlevel
            return (
                even * out[f, level, pl.ds(0, hrow, stride=2), :]
                + odd * out[f, level, pl.ds(1, hrow, stride=2), :]
            )

        tall = []
        for k in range(half):
            tall.append(jnp.concatenate([pairs(k), pairs(k + half)], axis=1))
        tall.append(jnp.concatenate([even + odd, jnp.zeros_like(even)], axis=1))
        piece[...] = jnp.dot(
            jnp.concatenate(tall, axis=0),
            gather,
            precision=lax.Precision.HIGHEST,
            preferred_element_type=jnp.float32,
        )

        @pl.when(domain == 1)
        def _():
            chosen[...] = piece[...]
            repeat(feeds, lambda flat: feed_one(flat).start())

        @pl.when(domain > 1)
        def _():
            swap().start()
            swap().wait_recv()
            mine = find_slot()[0] == parity * foot
            chosen[...] = jnp.where(mine, piece[...], swapped[...])
            repeat(places, lambda place: feed_slot(place).start())

    @pl.when(is_parent)
    def _():
        away = device(1, i // 2, j // 2)

        def take_one(flat):
            option = flat // places
            place = flat % places
            row_gap = i - 1 - option
            back = j - place

            @pl.when((row_gap >= 0) & (row_gap < foot) & (back >= 0) & (back < span))
            def _():
                for part in range(4):
                    copy(
                        chosen,
                        one_sums.at[flat, part],
                        feed_send.at[0],
                        one_recv.at[flat, part],
                        away,
                    ).wait_recv()

        def take_slot(place):
            back = j - place

            @pl.when((back >= 0) & (back < span))
            def _():
                for part in range(4):
                    copy(
                        chosen,
                        slot_sums.at[place, part],
                        feed_send.at[0],
                        slot_recv.at[place, part],
                        away,
                    ).wait_recv()

        repeat(feeds, take_one)
        repeat(places, take_slot)
        one_row = anchors[0, 0] // nrow
        one_col = anchors[1, 0] // ncol
        slot = i // foot
        second = anchors[0, 1] // nrow == slot * foot
        slot_col = jnp.where(second, anchors[1, 1], anchors[1, 2]) // ncol
        slot_at = jnp.clip(slot_col, 0, places - 1)
        one_in = (i >= one_row) & (i < one_row + foot) & (j >= one_col) & (j < one_col + span)
        slot_in = (j >= slot_col) & (j < slot_col + span)
        one_at = jnp.clip((one_row - 1) * places + one_col, 0, feeds - 1)
        left = lax.broadcasted_iota(jnp.int32, (hrow, ncol), 1) < hcol

        def both(part, rows):
            one = one_sums[one_at, part, rows, :]
            other = slot_sums[slot_at, part, rows, :]
            return jnp.where(one_in, one, 0.0) + jnp.where(slot_in, other, 0.0)

        for p in range(2):
            here = slice(p * hrow, (p + 1) * hrow)
            rows = slice(half * hrow, (half + 1) * hrow)
            total = jnp.where(
                left, both(2 * p, rows), pltpu.roll(both(2 * p + 1, rows), hcol, 1)
            )
            accept = (mask[here, :] == 1) & (total > 0.0)
            scale = 1.0 / jnp.maximum(total, 1.0)
            for k in range(half):
                rows = slice(k * hrow, (k + 1) * hrow)
                near = both(2 * p, rows)
                far = both(2 * p + 1, rows)
                low = jnp.where(left, near, pltpu.roll(far, hcol, 1))
                high = jnp.where(left, pltpu.roll(near, hcol, 1), far)
                for field, sums in ((k, low), (k + half, high)):
                    f, level = field // nlevel, field % nlevel
                    out[f, level, here, :] = jnp.where(
                        accept, sums * scale, current[0, f, level, here, :]
                    )

    halo(0, "send")

    @pl.when(is_parent)
    def _():
        for phase in range(2):
            for number in (1, 2, 3):
                tell(phase, number).wait_send()

    @pl.when(is_nest)
    def _():
        halo(1, "send")
        halo(2, "send")
        edges_out(0, "send")
        edges_out(1, "send")

        @pl.when(domain == 1)
        def _():
            repeat(feeds, lambda flat: feed_one(flat).wait_send())

        @pl.when(domain > 1)
        def _():
            swap().wait_send()
            repeat(places, lambda place: feed_slot(place).wait_send())


def shards(row_tiles, col_tiles, state, vert_mix, fb_mask, nu_coef, adv_coef, anchors):
    nfield, nlevel, nrow, ncol = state.shape
    count = nfield * nlevel
    padded = -(-count // 8) * 8
    foot = row_tiles // 4
    span = col_tiles // 2
    places = span + 1
    options = max(foot, 2)
    tall = (count // 2 + 1) * (nrow // 2)
    sent = 4 * foot * span
    f32 = jnp.float32
    vmem = pl.BlockSpec(memory_space=pltpu.VMEM)
    dma = pltpu.SemaphoreType.DMA
    return pl.pallas_call(
        functools.partial(kernel, row_tiles, col_tiles),
        out_shape=jax.ShapeDtypeStruct(state.shape, f32),
        in_specs=[pl.BlockSpec(memory_space=pl.ANY)] * 6,
        out_specs=vmem,
        scratch_shapes=[
            pltpu.VMEM(state.shape, f32),
            pltpu.VMEM((nrow, ncol), f32),
            pltpu.VMEM((nrow, ncol), jnp.int32),
            pltpu.SMEM((4, nlevel, nfield), f32),
            pltpu.SMEM((4, nlevel, nfield), f32),
            pltpu.SMEM((2, 3), jnp.int32),
            pltpu.VMEM((2, nfield, nlevel, nrow, ncol), f32),
            pltpu.VMEM((3, 2 * padded + nrow, ncol), f32),
            pltpu.VMEM((2, 2 * padded + nrow, ncol), f32),
            pltpu.VMEM((3, 2, padded, ncol), f32),
            pltpu.VMEM((3, 2, nrow, ncol), f32),
            pltpu.VMEM((options * places, padded, ncol), f32),
            pltpu.VMEM((options * places, padded, ncol), f32),
            pltpu.VMEM((options * places, nrow // 2, ncol), f32),
            pltpu.VMEM((options * places, nrow // 2, ncol), f32),
            pltpu.VMEM((2, padded, ncol), f32),
            pltpu.VMEM((2, nrow, ncol), f32),
            pltpu.VMEM((2, padded, ncol), f32),
            pltpu.VMEM((2, nrow, ncol), f32),
            pltpu.VMEM((2 * nlevel, nrow, ncol), f32),
            pltpu.VMEM((tall, ncol), f32),
            pltpu.VMEM((tall, ncol), f32),
            pltpu.VMEM((tall, ncol), f32),
            pltpu.VMEM((foot * places, 4, tall, ncol), f32),
            pltpu.VMEM((places, 4, tall, ncol), f32),
            dma((6,)),
            dma((3, 4)),
            dma((3, 4)),
            dma((2, 3)),
            dma((2,)),
            dma((2, 2, sent)),
            dma((2, 2, options * places)),
            dma((2,)),
            dma((foot * places,)),
            dma((foot * places, 4)),
            dma((places, 4)),
        ],
        compiler_params=pltpu.CompilerParams(
            has_side_effects=True, collective_id=0, vmem_limit_bytes=VMEM_LIMIT
        ),
    )(*[pltpu.with_memory_space_constraint(v, pltpu.HBM) for v in (
        state,
        vert_mix,
        fb_mask,
        jnp.swapaxes(nu_coef, 1, 2),
        jnp.swapaxes(adv_coef, 1, 2),
        jnp.swapaxes(anchors, 0, 1),
    )])


def solution(mesh):
    in_specs = (
        P(None, None, ("dom", "ty"), "tx"),
        P(("dom", "ty"), "tx"),
        P(("dom", "ty"), "tx"),
        P(),
        P(),
        P(),
    )
    out_specs = P(None, None, ("dom", "ty"), "tx")
    body = functools.partial(shards, mesh.shape["ty"], mesh.shape["tx"])
    return jax.shard_map(body, mesh=mesh, in_specs=in_specs, out_specs=out_specs, check_vma=False)
```

```python
import functools

import jax
import jax.numpy as jnp
from jax import lax
from jax.experimental import pallas as pl
from jax.experimental.pallas import tpu as pltpu
from jax.sharding import PartitionSpec as P

SUBSTEPS = 3
VMEM_LIMIT = 32 << 20
MESH = pl.DeviceIdType.MESH


def repeat(count, body):
    if count <= 4:
        for index in range(count):
            body(index)
    else:

        def step(index, carry):
            body(index)
            return carry

        lax.fori_loop(0, count, step, 0)


def kernel(
    row_tiles,
    col_tiles,
    whole,
    mix_in,
    mask_in,
    nu_in,
    adv_in,
    anchors_in,
    out,
    state,
    mix,
    mask,
    nu,
    adv,
    anchors,
    current,
    packs,
    held,
    side_packs,
    side_halos,
    halo_rows,
    halo_cols,
    old_rows,
    new_rows,
    old_cols,
    new_cols,
    spread_rows,
    spread_cols,
    ghost_rows,
    ghost_cols,
    coef,
    piece,
    swapped,
    chosen,
    one_sums,
    slot_sums,
    load_sem,
    halo_send,
    halo_recv,
    group_send,
    group_recv,
    tell_send,
    held_recv,
    edge_send,
    edge_recv,
    swap_sem,
    feed_send,
    one_recv,
    slot_recv,
):
    nfield, nlevel, nrow, ncol = state.shape
    count = nfield * nlevel
    padded = packs.shape[1] - nrow
    padded = padded // 2
    half = count // 2
    edge_rows, edge_cols = (old_rows, new_rows), (old_cols, new_cols)
    hrow, hcol = nrow // 2, ncol // 2
    half_rows = row_tiles // 2
    foot = half_rows // 2
    span = col_tiles // 2
    places = span + 1

    dom = lax.axis_index("dom")
    ty = lax.axis_index("ty")
    j = lax.axis_index("tx")
    parity = ty % 2
    i = ty // 2
    domain = 2 * dom + parity
    is_parent = domain == 0
    is_nest = domain > 0
    row_id = lax.broadcasted_iota(jnp.int32, (nrow, ncol), 0)
    lane = lax.broadcasted_iota(jnp.int32, (nrow, ncol), 1)

    def device(number, row, col):
        return (number // 2, 2 * row + number % 2, col)

    def copy(src, dst, send, recv, target):
        return pltpu.make_async_remote_copy(
            src_ref=src,
            dst_ref=dst,
            send_sem=send,
            recv_sem=recv,
            device_id=target,
            device_id_type=MESH,
        )

    loads = [
        pltpu.make_async_copy(source, target, load_sem.at[index])
        for index, (source, target) in enumerate(
            (
                (whole, state),
                (mix_in, mix),
                (mask_in, mask),
                (nu_in, nu),
                (adv_in, adv),
                (anchors_in, anchors),
            )
        )
    ]
    for load in loads:
        load.start()
    barrier = pltpu.get_barrier_semaphore()

    def greet(target):
        pl.semaphore_signal(barrier, inc=1, device_id=target, device_id_type=MESH)

    greeted = jnp.int32(0)
    for there, row, col in (
        (i > 0, i - 1, j),
        (i < half_rows - 1, i + 1, j),
        (j > 0, i, j - 1),
        (j < col_tiles - 1, i, j + 1),
    ):
        greeted = greeted + there.astype(jnp.int32)

        @pl.when(there)
        def _():
            greet(device(domain, row, col))

    inside = half_rows > 2 and col_tiles > 2

    def greet_sources(row):
        def one(place):
            col = place + j // 2

            @pl.when((row != i) | (col != j))
            def _():
                greet(device(domain, row, col))

        repeat(places, one)

    @pl.when(is_parent)
    def _():
        for number in (1, 2, 3):
            greet(device(number, i, j))

        def nests(number, row_start, back):
            row_gap = i - row_start
            place = j - back

            @pl.when((row_gap >= 0) & (row_gap < foot) & (place >= 0) & (place < places))
            def _():
                for p in range(2):
                    for q in range(2):
                        row, col = 2 * row_gap + p, 2 * back + q

                        @pl.when(
                            (row > 0) & (row < half_rows - 1) & (col > 0) & (col < col_tiles - 1)
                        )
                        def _():
                            greet(device(number, row, col))

        if inside:
            for number in (2, 3):
                repeat(span, lambda back, number=number: nests(number, (i // foot) * foot, back))
            repeat(foot * span, lambda flat: nests(1, 1 + flat // span, flat % span))

    @pl.when(domain == 1)
    def _():
        greet(device(0, i, j))
        repeat(foot, lambda option: greet_sources(1 + option + i // 2))

    @pl.when(domain > 1)
    def _():
        greet(device(0, i, j))
        greet((dom, 2 * i + 1 - parity, j))
        repeat(2, lambda option: greet_sources(option * foot + i // 2))

    def pack(load, phase):
        packed = jnp.zeros((nrow, ncol), jnp.float32)
        for k in range(count):
            cells = load(k // nlevel, k % nlevel)
            packs[phase, k : k + 1, :] = cells[0:1, :]
            packs[phase, padded + k : padded + k + 1, :] = cells[nrow - 1 : nrow, :]
            rolled = pltpu.roll(cells, 2 * k + 1, 1)
            packed = jnp.where((lane == 2 * k) | (lane == 2 * k + 1), rolled, packed)
        if padded > count:
            rest = jnp.zeros((padded - count, ncol), jnp.float32)
            packs[phase, count:padded, :] = rest
            packs[phase, padded + count : 2 * padded, :] = rest
        packs[phase, 2 * padded :, :] = packed

    split = 2
    groups = (range(split), range(split, nfield))
    spans = ((0, split * nlevel), (split * nlevel, padded - split * nlevel))

    def pack_group(load, phase, g):
        packed = jnp.zeros((nrow, ncol), jnp.float32)
        for f in groups[g]:
            for level in range(nlevel):
                k = f * nlevel + level
                cells = load(f, level)
                packs[phase, k : k + 1, :] = cells[0:1, :]
                packs[phase, padded + k : padded + k + 1, :] = cells[nrow - 1 : nrow, :]
                rolled = pltpu.roll(cells, 2 * k + 1, 1)
                packed = jnp.where((lane == 2 * k) | (lane == 2 * k + 1), rolled, packed)
        if g == 1 and padded > count:
            rest = jnp.zeros((padded - count, ncol), jnp.float32)
            packs[phase, count:padded, :] = rest
            packs[phase, padded + count : 2 * padded, :] = rest
        side_packs[phase - 1, g] = packed

    def halo_group(phase, g, act):
        start, size = spans[g]
        top, low = pl.ds(start, size), pl.ds(padded + start, size)
        down, up = i < half_rows - 1, i > 0
        right, left = j < col_tiles - 1, j > 0
        moves = (
            (0, down, packs.at[phase, low], halo_rows.at[phase, 0, top], i + 1, j, up),
            (1, up, packs.at[phase, top], halo_rows.at[phase, 1, top], i - 1, j, down),
            (2, right, side_packs.at[phase - 1, g], side_halos.at[phase - 1, g, 0], i, j + 1, left),
            (3, left, side_packs.at[phase - 1, g], side_halos.at[phase - 1, g, 1], i, j - 1, right),
        )
        for way, sends, source, dest, row, col, takes in moves:

            def go(source=source, dest=dest, row=row, col=col, way=way):
                return copy(
                    source,
                    dest,
                    group_send.at[phase - 1, g, way],
                    group_recv.at[phase - 1, g, way],
                    device(domain, row, col),
                )

            @pl.when(takes if act == "recv" else sends)
            def _():
                if act == "start":
                    go().start()
                elif act == "recv":
                    go().wait_recv()
                else:
                    go().wait_send()

    first_row = pl.ds(0, padded)
    last_row = pl.ds(padded, padded)
    side_cols = pl.ds(2 * padded, nrow)

    def halo(phase, act):
        moves = (
            (0, i < half_rows - 1, last_row, halo_rows, 0, i + 1, j, i > 0, i - 1, j),
            (1, i > 0, first_row, halo_rows, 1, i - 1, j, i < half_rows - 1, i + 1, j),
            (2, j < col_tiles - 1, side_cols, halo_cols, 0, i, j + 1, j > 0, i, j - 1),
            (3, j > 0, side_cols, halo_cols, 1, i, j - 1, j < col_tiles - 1, i, j + 1),
        )
        for way, sends, rows, buffer, side, row, col, takes, from_row, from_col in moves:

            def transfer(target, rows=rows, buffer=buffer, side=side, way=way):
                return copy(
                    packs.at[phase, rows],
                    buffer.at[phase, side],
                    halo_send.at[phase, way],
                    halo_recv.at[phase, way],
                    target,
                )

            if act == "start":

                @pl.when(sends)
                def _():
                    transfer(device(domain, row, col)).start()

            elif act == "recv":

                @pl.when(takes)
                def _():
                    transfer(device(domain, from_row, from_col)).wait_recv()

            else:

                @pl.when(sends)
                def _():
                    transfer(device(domain, row, col)).wait_send()

    def tell(phase, number):
        return copy(
            packs.at[phase],
            held.at[phase],
            tell_send.at[phase, number - 1],
            held_recv.at[phase],
            device(number, i, j),
        )

    def edges_out(phase, act):
        def one(option, row_start, back, index):
            row_gap = i - row_start
            place = j - back
            fits = (row_gap >= 0) & (row_gap < foot) & (place >= 0) & (place < places)
            slot = option * places + place
            for p in range(2):
                for q in range(2):
                    row = 2 * row_gap + p
                    col = 2 * back + q
                    here = (row == i) & (col == j)
                    spot = 4 * index + 2 * p + q

                    def go(rows, kind, buffer):
                        away = copy(
                            held.at[phase, rows],
                            buffer[phase].at[slot],
                            edge_send.at[phase, kind, spot],
                            edge_recv.at[phase, kind, slot],
                            device(domain, row, col),
                        )

                        @pl.when(jnp.logical_not(here))
                        def _():
                            if act == "start":
                                away.start()
                            else:
                                away.wait_send()

                        if act == "start":

                            @pl.when(here)
                            def _():
                                pltpu.make_async_copy(
                                    held.at[phase, rows],
                                    buffer[phase].at[slot],
                                    edge_recv.at[phase, kind, slot],
                                ).start()

                    @pl.when(fits & ((col == 0) | (col == col_tiles - 1)))
                    def _():
                        go(pl.ds(2 * padded + p * hrow, hrow), 1, edge_cols)

                    @pl.when(fits & (row == 0))
                    def _():
                        go(first_row, 0, edge_rows)

                    @pl.when(fits & (row == half_rows - 1))
                    def _():
                        go(last_row, 0, edge_rows)

        @pl.when(domain > 1)
        def _():
            option = i // foot
            repeat(span, lambda back: one(option, option * foot, back, back))

        @pl.when(domain == 1)
        def _():
            repeat(
                foot * span,
                lambda flat: one(flat // span, 1 + flat // span, flat % span, flat),
            )

    at_row_end = (i == 0) | (i == half_rows - 1)
    at_col_end = (j == 0) | (j == col_tiles - 1)
    def find_slot():
        number_here = jnp.maximum(domain - 1, 0)
        row_here = anchors[0, number_here] // nrow
        col_here = anchors[1, number_here] // ncol
        option_here = jnp.where(domain == 1, row_here - 1, row_here // foot)
        slot = option_here * places + col_here
        return row_here, jnp.clip(slot, 0, old_rows.shape[0] - 1)

    def edges_in(phase):
        def wait(slot):
            away = device(0, i // 2, j // 2)

            @pl.when(at_row_end)
            def _():
                copy(
                    packs.at[phase, first_row],
                    edge_rows[phase].at[slot],
                    edge_send.at[phase, 0, 0],
                    edge_recv.at[phase, 0, slot],
                    away,
                ).wait_recv()

            @pl.when(at_col_end)
            def _():
                copy(
                    packs.at[phase, pl.ds(2 * padded, hrow)],
                    edge_cols[phase].at[slot],
                    edge_send.at[phase, 1, 0],
                    edge_recv.at[phase, 1, slot],
                    away,
                ).wait_recv()

        @pl.when(domain == 1)
        def _():
            repeat(foot * places, wait)

        @pl.when(domain > 1)
        def _():
            repeat(2 * places, wait)

        row_here, slot_here = find_slot()

        @pl.when(at_row_end)
        def _():
            source = lax.broadcasted_iota(jnp.int32, (ncol, ncol), 0)
            target = lax.broadcasted_iota(jnp.int32, (ncol, ncol), 1)
            spread = (source == (j % 2) * hcol + target // 2).astype(jnp.float32)
            spread_rows[phase] = jnp.dot(
                edge_rows[phase][slot_here],
                spread,
                precision=lax.Precision.HIGHEST,
                preferred_element_type=jnp.float32,
            )

        @pl.when(at_col_end)
        def _():
            values = edge_cols[phase][slot_here]
            spread_cols[phase, pl.ds(0, hrow, stride=2), :] = values
            spread_cols[phase, pl.ds(1, hrow, stride=2), :] = values

    def ghosts_group(phase, g):
        start, size = spans[g]
        rows = slice(start, start + size)
        weight = phase / SUBSTEPS
        for side, inner in ((0, i > 0), (1, i < half_rows - 1)):

            @pl.when(inner)
            def _():
                ghost_rows[side, rows, :] = halo_rows[phase, side, rows, :]

            @pl.when(jnp.logical_not(inner))
            def _():
                old, new = spread_rows[0, rows, :], spread_rows[1, rows, :]
                ghost_rows[side, rows, :] = old + weight * (new - old)

        for side, inner in ((0, j > 0), (1, j < col_tiles - 1)):

            @pl.when(inner)
            def _():
                ghost_cols[side] = side_halos[phase - 1, g, side]

            if g == 0:

                @pl.when(jnp.logical_not(inner))
                def _():
                    shift = ncol - 1 if side == 0 else 1
                    old, new = spread_cols[0], spread_cols[1]
                    ghost_cols[side] = pltpu.roll(old + weight * (new - old), shift, 1)

    def ghosts(phase):
        def blended(values):
            return values[0]

        for side, inner in ((0, i > 0), (1, i < half_rows - 1)):

            @pl.when(inner)
            def _():
                ghost_rows[side] = halo_rows[phase, side]

            @pl.when(jnp.logical_not(inner) & is_nest)
            def _():
                ghost_rows[side] = blended(spread_rows)

            @pl.when(jnp.logical_not(inner) & is_parent)
            def _():
                ghost_rows[side] = jnp.zeros((padded, ncol), jnp.float32)

        for side, inner in ((0, j > 0), (1, j < col_tiles - 1)):

            @pl.when(inner)
            def _():
                ghost_cols[side] = halo_cols[phase, side]

            @pl.when(jnp.logical_not(inner) & is_nest)
            def _():
                shift = ncol - 1 if side == 0 else 1
                ghost_cols[side] = pltpu.roll(blended(spread_cols), shift, 1)

            @pl.when(jnp.logical_not(inner) & is_parent)
            def _():
                ghost_cols[side] = jnp.zeros((nrow, ncol), jnp.float32)

    def advance(load, store, fields=range(nfield)):
        sides = jnp.where(lane % 2 == 0, ghost_cols[0], ghost_cols[1])
        mixing = mix[...]
        for f in fields:
            forward = []
            for level in range(nlevel):
                k = f * nlevel + level
                cells = load(f, level)
                diffusion = nu[domain, level, f]
                advection = adv[domain, level, f]
                above = jnp.where(
                    row_id == 0, ghost_rows[0, k : k + 1, :], pltpu.roll(cells, 1, 0)
                )
                below = jnp.where(
                    row_id == nrow - 1,
                    ghost_rows[1, k : k + 1, :],
                    pltpu.roll(cells, nrow - 1, 0),
                )
                beside = pltpu.roll(sides, (ncol - 2 * k - 1) % ncol, 1)
                west = pltpu.roll(jnp.where(lane == ncol - 1, beside, cells), 1, 1)
                east = pltpu.roll(jnp.where(lane == 0, beside, cells), ncol - 1, 1)
                explicit = (
                    cells
                    + diffusion * (above + below + west + east - 4.0 * cells)
                    + advection * (west - cells)
                )
                if level == 0:
                    forward.append(explicit * coef[level])
                else:
                    forward.append((explicit + mixing * forward[-1]) * coef[level])
            solved = forward[-1]
            store(f, nlevel - 1, solved)
            for level in range(nlevel - 2, -1, -1):
                solved = forward[level] + coef[nlevel + level] * solved
                store(f, level, solved)

    def put(buffer, *prefix):
        def store(f, level, values):
            buffer[(*prefix, f, level)] = values

        return store

    def get(buffer, *prefix):
        return lambda f, level: buffer[(*prefix, f, level)]

    for load in loads[1:]:
        load.wait()
    mixing = mix[...]
    ratio = None
    for level in range(nlevel):
        ends = (1.0 if level == 0 else 0.0) + (1.0 if level == nlevel - 1 else 0.0)
        pivot = 1.0 + mixing * (2.0 - ends)
        if level > 0:
            pivot = pivot - mixing * ratio
        inverse = 1.0 / pivot
        ratio = mixing * inverse
        coef[level] = inverse
        coef[nlevel + level] = ratio

    loads[0].wait()
    pack(get(state), 0)
    backs = jnp.minimum(span - 1, j) - jnp.maximum(0, j - span) + 1
    gaps = jnp.minimum(foot - 1, i - 1) - jnp.maximum(0, i - foot) + 1
    option_start = (i // foot) * foot
    lone = jnp.where(domain == 1, i >= 1, option_start == i - i // 2).astype(jnp.int32)
    targets = 4 * backs * jnp.where(domain == 1, gaps, 1) - lone
    if inside:
        deep = jnp.logical_not(at_row_end | at_col_end).astype(jnp.int32)
        targets = targets + deep * places * jnp.where(domain == 1, foot, 2)
    partners = jnp.where(is_parent, 3, 1 + targets + jnp.where(domain == 1, 0, 1))
    pl.semaphore_wait(barrier, greeted + partners)

    def relay(phase):
        tell(phase, 1).wait_recv()
        edges_out(phase, "start")

    @pl.when(is_parent)
    def _():
        for number in (2, 3, 1):
            tell(0, number).start()

    halo(0, "start")

    @pl.when(is_nest)
    def _():
        relay(0)

    halo(0, "recv")

    @pl.when(is_nest)
    def _():
        relay(1)
        edges_in(0)

    ghosts(0)

    @pl.when(is_nest)
    def _():
        for g in range(2):
            advance(get(state), put(current, 0), groups[g])
            pack_group(get(current, 0), 1, g)
            halo_group(1, g, "start")

    @pl.when(is_parent)
    def _():
        advance(get(state), put(current, 0))
        pack(get(current, 0), 1)
        for number in (2, 3, 1):
            tell(1, number).start()

    feeds = foot * places
    home = j - j // 2

    def far_first(step):
        down = (home - 1 - step + places) % places
        return jnp.where(j < span, down, (home + 1 + step) % places)

    def cut_of(ref, chunk):
        return ref.at[pl.ds(0, half * hrow) if chunk == 0 else pl.ds(half * hrow, hrow)]

    def feed_one(flat, chunk):
        option = flat // places
        place = flat % places
        where_to = device(0, 1 + option + i // 2, place + j // 2)
        part = 2 * (i % 2) + j % 2
        return copy(
            cut_of(piece, chunk),
            cut_of(one_sums.at[flat, part], chunk),
            feed_send.at[chunk, flat],
            one_recv.at[chunk, flat, part],
            where_to,
        )

    def feed_ones(chunk):
        repeat(
            feeds,
            lambda step: feed_one(step // places * places + far_first(step % places), chunk).start(),
        )

    def feed_slot(place, chunk):
        where_to = device(0, parity * foot + i // 2, place + j // 2)
        part = 2 * (i % 2) + j % 2
        return copy(
            cut_of(chosen, chunk),
            cut_of(slot_sums.at[place, part], chunk),
            feed_send.at[chunk, place],
            slot_recv.at[chunk, place, part],
            where_to,
        )

    def swap(chunk):
        return copy(
            cut_of(piece, chunk),
            cut_of(swapped, chunk),
            swap_sem.at[chunk, 0],
            swap_sem.at[chunk, 1],
            (dom, 2 * i + 1 - parity, j),
        )

    def feed_slots(chunk):
        mine = find_slot()[0] == parity * foot
        swap(chunk).wait_recv()
        part = cut_of(chosen, chunk)
        part[...] = jnp.where(mine, cut_of(piece, chunk)[...], cut_of(swapped, chunk)[...])
        repeat(places, lambda step: feed_slot(far_first(step), chunk).start())

    @pl.when(is_nest)
    def _():
        source = lax.broadcasted_iota(jnp.int32, (2 * ncol, ncol), 0)
        target = lax.broadcasted_iota(jnp.int32, (2 * ncol, ncol), 1)
        gather = (target == source // 2).astype(jnp.float32)
        even = mask[pl.ds(0, hrow, stride=2), :].astype(jnp.float32)
        odd = mask[pl.ds(1, hrow, stride=2), :].astype(jnp.float32)

        def offer(chunk, blocks):
            part = cut_of(piece, chunk)
            part[...] = jnp.dot(
                jnp.concatenate(blocks, axis=0),
                gather,
                precision=lax.Precision.HIGHEST,
                preferred_element_type=jnp.float32,
            )

            @pl.when(domain == 1)
            def _():
                feed_ones(chunk)

            @pl.when(domain > 1)
            def _():
                swap(chunk).start()

        offer(1, [jnp.concatenate([even + odd, jnp.zeros_like(even)], axis=1)])
        edges_in(1)
        for g in range(2):
            halo_group(1, g, "recv")
            ghosts_group(1, g)
            advance(get(current, 0), put(current, 1), groups[g])
            pack_group(get(current, 1), 2, g)
            halo_group(2, g, "start")

        @pl.when(domain > 1)
        def _():
            feed_slots(1)

        for g in range(2):
            halo_group(2, g, "recv")
            ghosts_group(2, g)
            advance(get(current, 1), put(out), groups[g])

        def weighed(k):
            f, level = k // nlevel, k % nlevel
            return (
                even * out[f, level, pl.ds(0, hrow, stride=2), :]
                + odd * out[f, level, pl.ds(1, hrow, stride=2), :]
            )

        offer(
            0,
            [jnp.concatenate([weighed(k), weighed(k + half)], axis=1) for k in range(half)],
        )

        @pl.when(domain > 1)
        def _():
            feed_slots(0)

    @pl.when(is_parent)
    def _():
        away = device(1, i // 2, j // 2)

        def take_one(flat, chunk):
            option = flat // places
            place = flat % places
            row_gap = i - 1 - option
            back = j - place

            @pl.when((row_gap >= 0) & (row_gap < foot) & (back >= 0) & (back < span))
            def _():
                for part in range(4):
                    copy(
                        cut_of(piece, chunk),
                        cut_of(one_sums.at[flat, part], chunk),
                        feed_send.at[chunk, 0],
                        one_recv.at[chunk, flat, part],
                        away,
                    ).wait_recv()

        def take_slot(place, chunk):
            back = j - place

            @pl.when((back >= 0) & (back < span))
            def _():
                for part in range(4):
                    copy(
                        cut_of(chosen, chunk),
                        cut_of(slot_sums.at[place, part], chunk),
                        feed_send.at[chunk, 0],
                        slot_recv.at[chunk, place, part],
                        away,
                    ).wait_recv()

        for chunk in (1, 0):
            repeat(feeds, lambda flat: take_one(flat, chunk))
            repeat(places, lambda place: take_slot(place, chunk))
        one_row = anchors[0, 0] // nrow
        one_col = anchors[1, 0] // ncol
        slot = i // foot
        second = anchors[0, 1] // nrow == slot * foot
        slot_col = jnp.where(second, anchors[1, 1], anchors[1, 2]) // ncol
        slot_at = jnp.clip(slot_col, 0, places - 1)
        one_in = (i >= one_row) & (i < one_row + foot) & (j >= one_col) & (j < one_col + span)
        slot_in = (j >= slot_col) & (j < slot_col + span)
        one_at = jnp.clip((one_row - 1) * places + one_col, 0, feeds - 1)
        left = lax.broadcasted_iota(jnp.int32, (hrow, ncol), 1) < hcol

        def both(part, rows):
            one = one_sums[one_at, part, rows, :]
            other = slot_sums[slot_at, part, rows, :]
            return jnp.where(one_in, one, 0.0) + jnp.where(slot_in, other, 0.0)

        for p in range(2):
            here = slice(p * hrow, (p + 1) * hrow)
            rows = slice(half * hrow, (half + 1) * hrow)
            total = jnp.where(
                left, both(2 * p, rows), pltpu.roll(both(2 * p + 1, rows), hcol, 1)
            )
            accept = (mask[here, :] == 1) & (total > 0.0)
            scale = 1.0 / jnp.maximum(total, 1.0)
            for k in range(half):
                rows = slice(k * hrow, (k + 1) * hrow)
                near = both(2 * p, rows)
                far = both(2 * p + 1, rows)
                low = jnp.where(left, near, pltpu.roll(far, hcol, 1))
                high = jnp.where(left, pltpu.roll(near, hcol, 1), far)
                for field, sums in ((k, low), (k + half, high)):
                    f, level = field // nlevel, field % nlevel
                    out[f, level, here, :] = jnp.where(
                        accept, sums * scale, current[0, f, level, here, :]
                    )

    halo(0, "send")

    @pl.when(is_parent)
    def _():
        for phase in range(2):
            for number in (1, 2, 3):
                tell(phase, number).wait_send()

    @pl.when(is_nest)
    def _():
        for g in range(2):
            halo_group(1, g, "send")
            halo_group(2, g, "send")
        edges_out(0, "send")
        edges_out(1, "send")

        @pl.when(domain == 1)
        def _():
            for chunk in range(2):
                repeat(feeds, lambda flat: feed_one(flat, chunk).wait_send())

        @pl.when(domain > 1)
        def _():
            for chunk in range(2):
                swap(chunk).wait_send()
                repeat(places, lambda place: feed_slot(place, chunk).wait_send())


def shards(row_tiles, col_tiles, state, vert_mix, fb_mask, nu_coef, adv_coef, anchors):
    nfield, nlevel, nrow, ncol = state.shape
    count = nfield * nlevel
    padded = -(-count // 8) * 8
    foot = row_tiles // 4
    span = col_tiles // 2
    places = span + 1
    options = max(foot, 2)
    tall = (count // 2 + 1) * (nrow // 2)
    sent = 4 * foot * span
    f32 = jnp.float32
    vmem = pl.BlockSpec(memory_space=pltpu.VMEM)
    dma = pltpu.SemaphoreType.DMA
    return pl.pallas_call(
        functools.partial(kernel, row_tiles, col_tiles),
        out_shape=jax.ShapeDtypeStruct(state.shape, f32),
        in_specs=[pl.BlockSpec(memory_space=pl.ANY)] * 6,
        out_specs=vmem,
        scratch_shapes=[
            pltpu.VMEM(state.shape, f32),
            pltpu.VMEM((nrow, ncol), f32),
            pltpu.VMEM((nrow, ncol), jnp.int32),
            pltpu.SMEM((4, nlevel, nfield), f32),
            pltpu.SMEM((4, nlevel, nfield), f32),
            pltpu.SMEM((2, 3), jnp.int32),
            pltpu.VMEM((2, nfield, nlevel, nrow, ncol), f32),
            pltpu.VMEM((3, 2 * padded + nrow, ncol), f32),
            pltpu.VMEM((2, 2 * padded + nrow, ncol), f32),
            pltpu.VMEM((2, 2, nrow, ncol), f32),
            pltpu.VMEM((2, 2, 2, nrow, ncol), f32),
            pltpu.VMEM((3, 2, padded, ncol), f32),
            pltpu.VMEM((1, 2, nrow, ncol), f32),
            pltpu.VMEM((options * places, padded, ncol), f32),
            pltpu.VMEM((options * places, padded, ncol), f32),
            pltpu.VMEM((options * places, nrow // 2, ncol), f32),
            pltpu.VMEM((options * places, nrow // 2, ncol), f32),
            pltpu.VMEM((2, padded, ncol), f32),
            pltpu.VMEM((2, nrow, ncol), f32),
            pltpu.VMEM((2, padded, ncol), f32),
            pltpu.VMEM((2, nrow, ncol), f32),
            pltpu.VMEM((2 * nlevel, nrow, ncol), f32),
            pltpu.VMEM((tall, ncol), f32),
            pltpu.VMEM((tall, ncol), f32),
            pltpu.VMEM((tall, ncol), f32),
            pltpu.VMEM((foot * places, 4, tall, ncol), f32),
            pltpu.VMEM((places, 4, tall, ncol), f32),
            dma((6,)),
            dma((1, 4)),
            dma((1, 4)),
            dma((2, 2, 4)),
            dma((2, 2, 4)),
            dma((2, 3)),
            dma((2,)),
            dma((2, 2, sent)),
            dma((2, 2, options * places)),
            dma((2, 2)),
            dma((2, foot * places)),
            dma((2, foot * places, 4)),
            dma((2, places, 4)),
        ],
        compiler_params=pltpu.CompilerParams(
            has_side_effects=True, collective_id=0, vmem_limit_bytes=VMEM_LIMIT
        ),
    )(*[pltpu.with_memory_space_constraint(v, pltpu.HBM) for v in (
        state,
        vert_mix,
        fb_mask,
        jnp.swapaxes(nu_coef, 1, 2),
        jnp.swapaxes(adv_coef, 1, 2),
        jnp.swapaxes(anchors, 0, 1),
    )])


def solution(mesh):
    in_specs = (
        P(None, None, ("dom", "ty"), "tx"),
        P(("dom", "ty"), "tx"),
        P(("dom", "ty"), "tx"),
        P(),
        P(),
        P(),
    )
    out_specs = P(None, None, ("dom", "ty"), "tx")
    body = functools.partial(shards, mesh.shape["ty"], mesh.shape["tx"])
    return jax.shard_map(body, mesh=mesh, in_specs=in_specs, out_specs=out_specs, check_vma=False)
```
